128 devices in a mesh: space: 64 (over x, y, z), sub: 2 (over core).
Axes of the slice: x: 4, y: 4, z: 4, core: 2. Of those that a mesh axis runs over, the one named last changes fastest.
Arguments:
- mode_rows: float32 [256, 1048576], P(None, ('space', 'sub')), as said below
- snapshots: float32 [3, 64, 1048576], P(None, None, ('space', 'sub')), as said below
- probe_fields: float32 [128, 1048576], P(None, ('space', 'sub')), as said below
- core_factor: float32 [256, 256], replicated, as said below
Outputs:
- new_modes: float32 [256, 1048576], P(None, ('space', 'sub'))
- new_core: float32 [256, 256], replicated
- captured: float32 [3, 256, 320], replicated
Inputs may be any that keep to these rules, and one draw needn't show every extreme that they name: `mode_rows`: rows of full rank, entries of order one. `snapshots`: fields of order one. `probe_fields`: fields of order one. `core_factor`: lower triangular with a positive diagonal.
All inputs are finite; a program needn't handle non-finite values.
Results may differ from the reference program's by a relative error of at most 0.0003.
Values sent between devices are 32-bit elements; how exact they have to be, the bound alone decides.
A program may use at most 128 MiB of HBM per device.

```python
import jax
import jax.numpy as jnp
from jax import lax

K = 256
BATCH = 64
BATCHES = 3
PROBES = 128
TURNS = 2
ROWS = 1048576


DECAY_END = 0.03


NOISE_SIZE = 0.2


def shared_modes(key):
    return jax.random.normal(jax.random.fold_in(key, 11), (K, ROWS), jnp.float32)


def shared_fields(key):
    field_count = BATCH * 3 // 2
    return jax.random.normal(jax.random.fold_in(key, 13), (field_count, ROWS), jnp.float32)


def mixed_fields(key, salt, number):
    basis_all = shared_modes(key)
    fields = shared_fields(key)
    field_count = fields.shape[0]
    branch_key = jax.random.fold_in(key, salt)
    picked = jax.random.randint(jax.random.fold_in(branch_key, 1), (number, 4), 0, K)
    amounts = jax.random.normal(jax.random.fold_in(branch_key, 2), (number, 4), jnp.float32)
    steps_along = jnp.arange(field_count, dtype=jnp.float32) / (field_count - 1)
    decay = jnp.exp(steps_along * jnp.log(DECAY_END))
    decay = decay / jnp.sqrt(jnp.sum(decay * decay))
    mixing = jax.random.normal(jax.random.fold_in(branch_key, 4), (number, field_count), jnp.float32) * decay[None, :]
    summed = jax.random.normal(jax.random.fold_in(branch_key, 3), (number, ROWS), jnp.float32) * NOISE_SIZE
    summed = summed + jnp.dot(mixing, fields, precision=lax.Precision.HIGHEST)
    for member in range(4):
        summed = summed + amounts[:, member:member + 1] * basis_all[picked[:, member]]
    return summed


def draw_mode_rows(key, part):
    return shared_modes(key)


def draw_snapshots(key, part):
    return mixed_fields(key, 23, BATCHES * BATCH).reshape(BATCHES, BATCH, ROWS)


def draw_probe_fields(key, part):
    return mixed_fields(key, 37, PROBES)


def draw_core_factor(key, part):
    lowest = jnp.tril(jax.random.normal(jax.random.fold_in(key, 5), (K, K), jnp.float32), -1) * (0.5 / K ** 0.5)
    logs = jax.random.uniform(jax.random.fold_in(key, 6), (K,), jnp.float32, jnp.log(0.5), jnp.log(4.0))
    return lowest + jnp.diag(jnp.exp(logs))


def setup_inputs(seed: int = 0) -> dict:
    seeds = jax.random.split(jax.random.key(seed), 5)
    mode_rows = draw_mode_rows(jax.random.fold_in(seeds[4], 71), 0)
    snapshots = draw_snapshots(jax.random.fold_in(seeds[4], 71), 0)
    probe_fields = draw_probe_fields(jax.random.fold_in(seeds[4], 71), 0)
    core_factor = draw_core_factor(jax.random.fold_in(seeds[4], 71), 0)
    return {"mode_rows": mode_rows, "snapshots": snapshots, "probe_fields": probe_fields, "core_factor": core_factor}


PRECISE = lax.Precision.HIGHEST

def row_inner(left, right):
    return lax.dot_general(left, right, (((1,), (1,)), ((), ())), precision=PRECISE)

def matmul_high(left, right):
    return jnp.dot(left, right, precision=PRECISE)

def update_core(core_now, projected, factor):
    rank_count = core_now.shape[0]
    batch_count = factor.shape[0]
    upper = jnp.concatenate([core_now, projected], axis=1)
    bottom = jnp.concatenate([jnp.zeros((batch_count, rank_count), jnp.float32), factor.T], axis=1)
    stacked = jnp.concatenate([upper, bottom], axis=0)
    squared = matmul_high(stacked, stacked.T)
    rotation = jnp.eye(rank_count + batch_count, rank_count, dtype=jnp.float32)
    for sweep_index in range(TURNS):
        rotation = matmul_high(squared, rotation)
        lowered = jnp.linalg.cholesky(matmul_high(rotation.T, rotation))
        rotation = jax.scipy.linalg.solve_triangular(lowered, rotation.T, lower=True).T
    fresh_core = jnp.linalg.cholesky(matmul_high(rotation.T, matmul_high(squared, rotation)))
    return (rotation, fresh_core)

def reference(mode_rows, snapshots, probe_fields, core_factor):
    volume = 1.0 / ROWS
    window = jnp.concatenate([snapshots.reshape(BATCHES * BATCH, ROWS), probe_fields], axis=0)
    captured = []
    basis_now = mode_rows
    core_now = core_factor
    for batch_index in range(BATCHES):
        incoming = snapshots[batch_index]
        projected = row_inner(basis_now, incoming) * volume
        residual = incoming - matmul_high(projected.T, basis_now)
        factor = jnp.linalg.cholesky(row_inner(residual, residual) * volume)
        orthogonal = jax.scipy.linalg.solve_triangular(factor, residual, lower=True)
        rotation, core_now = update_core(core_now, projected, factor)
        basis_now = matmul_high(rotation.T, jnp.concatenate([basis_now, orthogonal], axis=0))
        captured.append(row_inner(basis_now, window) * volume)
    return (basis_now, core_now, jnp.stack(captured))
```

```python
import jax
import jax.numpy as jnp
from jax import lax
from jax.experimental import pallas as pl
from jax.experimental.pallas import tpu as pltpu
from jax.sharding import PartitionSpec as P

TURNS = 2
BLOCK = 64
PRECISE = lax.Precision.HIGHEST
SPLIT = lax.Precision.HIGH
AXES = ("space", "sub")


def dot_nn(left, right):
    return lax.dot_general(
        left, right, (((1,), (0,)), ((), ())), precision=PRECISE, preferred_element_type=jnp.float32
    )


def dot_nt(left, right):
    return lax.dot_general(
        left, right, (((1,), (1,)), ((), ())), precision=PRECISE, preferred_element_type=jnp.float32
    )


def inverse_root(value):
    guess = lax.rsqrt(value)
    return guess * (1.5 - 0.5 * value * guess * guess)


def factor_block(block):
    size = block.shape[0]
    row_ids = lax.broadcasted_iota(jnp.int32, (size, size), 0)
    col_ids = lax.broadcasted_iota(jnp.int32, (size, size), 1)
    identity = jnp.where(row_ids == col_ids, 1.0, 0.0).astype(jnp.float32)
    wide = jnp.concatenate([block, identity], axis=1)
    width = wide.shape[1]
    groups = size // 8
    tiles = [wide[8 * g:8 * g + 8, :] for g in range(groups)]
    sublane = lax.broadcasted_iota(jnp.int32, (8, width), 0)
    shape = (8, width)
    for g in range(groups):
        columns = {}
        for v in range(g, groups):
            columns[v] = [
                jnp.broadcast_to(tiles[v][:, 8 * g + j:8 * g + j + 1], shape) for j in range(8)
            ]
        pivots = [
            [jnp.broadcast_to(columns[g][j][i:i + 1, :], shape) for j in range(i + 1)]
            for i in range(8)
        ]
        rows = [jnp.broadcast_to(tiles[g][i:i + 1, :], shape) for i in range(8)]
        merged = jnp.zeros(shape, jnp.float32)
        for k in range(8):
            inv = inverse_root(pivots[k][k])
            done = rows[k] * inv
            merged = jnp.where(sublane == k, done, merged)
            lower = {i: pivots[i][k] * inv for i in range(k + 1, 8)}
            for i in range(k + 1, 8):
                rows[i] = rows[i] - lower[i] * done
                for j in range(k + 1, i + 1):
                    pivots[i][j] = pivots[i][j] - lower[i] * lower[j]
            for v in range(g + 1, groups):
                scaled = columns[v][k] * inv
                for j in range(k + 1, 8):
                    columns[v][j] = columns[v][j] - scaled * lower[j]
                tiles[v] = tiles[v] - scaled * done
        tiles[g] = merged
    both = jnp.concatenate(tiles, axis=0)
    upper = jnp.where(row_ids <= col_ids, both[:, :size], 0.0)
    return upper, both[:, size:]


def factor_solve(matrix, right, work, keep_factor=False):
    order = matrix.shape[0]
    count = right.shape[1] if right is not None else 0
    work[:order, :order] = matrix
    if count:
        work[:order, order:order + count] = right
    for start in range(0, order, BLOCK):
        stop = start + BLOCK
        first = start // 128 * 128
        last = order + count
        panel = work[start:stop, first:last]
        upper, inverse = factor_block(panel[:, start - first:stop - first])
        solved = dot_nn(inverse, panel)
        if stop < order:
            below = work[stop:order, start:stop]
            lower = dot_nt(below, inverse)
            work[stop:order, first:last] = work[stop:order, first:last] - dot_nn(lower, solved)
        work[start:stop, first:last] = solved
        if keep_factor:
            work[start:stop, start:stop] = upper
            if start:
                work[start:stop, :start] = jnp.zeros((BLOCK, start), jnp.float32)
    if count:
        return work[:order, order:order + count]
    return work[:order, :order]


def chain(modes, batches, batch, span, start_ref, core_ref, mix_ref, upper_ref, captured_ref,
          state, squared_ref, work):
    state[...] = start_ref[:modes, :]
    energy = dot_nt(core_ref[...], core_ref[...])
    window_at = span + modes
    window = captured_ref.shape[2]
    for b in range(batches):
        at = window_at + batch * b
        base = modes + batch * b
        projected = state[:, at:at + batch]
        residual = start_ref[base:base + batch, :] - dot_nn(projected.T, state[...])
        against = dot_nt(residual[:, span:2 * span], state[:, :span])
        gram = residual[:, at:at + batch] - dot_nn(against, projected)
        upper, inverse = factor_block(gram)
        orthogonal = dot_nn(inverse, residual)
        squared_ref[:modes, :modes] = energy + dot_nt(projected, projected)
        squared_ref[:modes, modes:] = dot_nt(projected, upper)
        squared_ref[modes:, :modes] = dot_nt(upper, projected)
        squared_ref[modes:, modes:] = dot_nt(upper, upper)
        turned = squared_ref[:modes, :]
        for turn in range(TURNS):
            if turn:
                turned = dot_nn(turned, squared_ref[...])
            turned = factor_solve(dot_nt(turned, turned), turned, work)
        energy = dot_nt(dot_nn(turned, squared_ref[...]), turned)
        state[...] = dot_nn(turned[:, :modes], state[...]) + dot_nn(turned[:, modes:], orthogonal)
        captured_ref[b] = state[:, window_at:window_at + window]
    mix_ref[...] = state[:, :span]
    upper_ref[...] = factor_solve(energy, None, work, keep_factor=True)


def body(mode_rows, snapshots, probe_fields, core_factor):
    modes, local_rows = mode_rows.shape
    batches, batch = snapshots.shape[:2]
    probes = probe_fields.shape[0]
    volume = 1.0 / (local_rows * lax.axis_size("space") * lax.axis_size("sub"))
    taken = batches * batch
    flat = snapshots.reshape(taken, local_rows)

    def inner(left, right):
        return lax.dot_general(left, right, (((1,), (1,)), ((), ())), precision=SPLIT)

    uu, uc, up, cc, cp = lax.psum(
        (
            inner(mode_rows, mode_rows),
            inner(mode_rows, flat),
            inner(mode_rows, probe_fields),
            inner(flat, flat),
            inner(flat, probe_fields),
        ),
        AXES,
    )
    total = modes + taken
    span = -(-total // 128) * 128
    gram = jnp.concatenate(
        [
            jnp.concatenate([uu, uc, up], axis=1),
            jnp.concatenate([uc.T, cc, cp], axis=1),
        ],
        axis=0,
    ) * volume
    width = -(-(total + probes) // 128) * 128
    start = jnp.concatenate(
        [
            jnp.eye(total, span, dtype=jnp.float32),
            jnp.pad(gram, ((0, 0), (0, width - total - probes))),
        ],
        axis=1,
    )
    vmem = pl.BlockSpec(memory_space=pltpu.VMEM)
    mix, upper, captured = pl.pallas_call(
        lambda *refs: chain(modes, batches, batch, span, *refs),
        out_shape=(
            jax.ShapeDtypeStruct((modes, span), jnp.float32),
            jax.ShapeDtypeStruct((modes, modes), jnp.float32),
            jax.ShapeDtypeStruct((batches, modes, taken + probes), jnp.float32),
        ),
        in_specs=[vmem, vmem],
        out_specs=(vmem, vmem, vmem),
        scratch_shapes=[
            pltpu.VMEM((modes, span + width), jnp.float32),
            pltpu.VMEM((modes + batch, modes + batch), jnp.float32),
            pltpu.VMEM((modes, 2 * modes + batch), jnp.float32),
        ],
        name="chain",
    )(start, core_factor)
    new_modes = jnp.dot(mix[:, :modes], mode_rows, precision=SPLIT) + jnp.dot(
        mix[:, modes:total], flat, precision=SPLIT
    )
    return (new_modes, upper.T, captured)


def solution(mesh):
    return jax.shard_map(
        body,
        mesh=mesh,
        in_specs=(
            P(None, AXES),
            P(None, None, AXES),
            P(None, AXES),
            P(),
        ),
        out_specs=(P(None, AXES), P(), P()),
        check_vma=False,
    )
```

```python
import jax
import jax.numpy as jnp
from jax import lax
from jax.experimental import pallas as pl
from jax.experimental.pallas import tpu as pltpu
from jax.sharding import PartitionSpec as P

TURNS = 2
BLOCK = 64
PRECISE = lax.Precision.HIGHEST
SPLIT = lax.Precision.HIGH
AXES = ("space", "sub")


def dot_nn(left, right):
    return lax.dot_general(
        left, right, (((1,), (0,)), ((), ())), precision=PRECISE, preferred_element_type=jnp.float32
    )


def dot_nt(left, right):
    return lax.dot_general(
        left, right, (((1,), (1,)), ((), ())), precision=PRECISE, preferred_element_type=jnp.float32
    )


def inverse_root(value):
    guess = lax.rsqrt(value)
    return guess * (1.5 - 0.5 * value * guess * guess)


def factor_block(block):
    size = block.shape[0]
    row_ids = lax.broadcasted_iota(jnp.int32, (size, size), 0)
    col_ids = lax.broadcasted_iota(jnp.int32, (size, size), 1)
    identity = jnp.where(row_ids == col_ids, 1.0, 0.0).astype(jnp.float32)
    wide = jnp.concatenate([block, identity], axis=1)
    width = wide.shape[1]
    groups = size // 8
    tiles = [wide[8 * g:8 * g + 8, :] for g in range(groups)]
    sublane = lax.broadcasted_iota(jnp.int32, (8, width), 0)
    shape = (8, width)
    for g in range(groups):
        columns = {}
        for v in range(g, groups):
            columns[v] = [
                jnp.broadcast_to(tiles[v][:, 8 * g + j:8 * g + j + 1], shape) for j in range(8)
            ]
        pivots = [
            [jnp.broadcast_to(columns[g][j][i:i + 1, :], shape) for j in range(i + 1)]
            for i in range(8)
        ]
        rows = [jnp.broadcast_to(tiles[g][i:i + 1, :], shape) for i in range(8)]
        merged = jnp.zeros(shape, jnp.float32)
        for k in range(8):
            inv = inverse_root(pivots[k][k])
            done = rows[k] * inv
            merged = jnp.where(sublane == k, done, merged)
            lower = {i: pivots[i][k] * inv for i in range(k + 1, 8)}
            for i in range(k + 1, 8):
                rows[i] = rows[i] - lower[i] * done
                for j in range(k + 1, i + 1):
                    pivots[i][j] = pivots[i][j] - lower[i] * lower[j]
            for v in range(g + 1, groups):
                scaled = columns[v][k] * inv
                for j in range(k + 1, 8):
                    columns[v][j] = columns[v][j] - scaled * lower[j]
                tiles[v] = tiles[v] - scaled * done
        tiles[g] = merged
    both = jnp.concatenate(tiles, axis=0)
    upper = jnp.where(row_ids <= col_ids, both[:, :size], 0.0)
    return upper, both[:, size:]


def factor_solve(matrix, right, work, keep_factor=False):
    order = matrix.shape[0]
    count = right.shape[1] if right is not None else 0
    work[:order, :order] = matrix
    if count:
        work[:order, order:order + count] = right
    for start in range(0, order, BLOCK):
        stop = start + BLOCK
        first = start // 128 * 128
        last = order + count
        panel = work[start:stop, first:last]
        upper, inverse = factor_block(panel[:, start - first:stop - first])
        solved = dot_nn(inverse, panel)
        if stop < order:
            below = work[stop:order, start:stop]
            lower = dot_nt(below, inverse)
            work[stop:order, first:last] = work[stop:order, first:last] - dot_nn(lower, solved)
        work[start:stop, first:last] = solved
        if keep_factor:
            work[start:stop, start:stop] = upper
            if start:
                work[start:stop, :start] = jnp.zeros((BLOCK, start), jnp.float32)
    if count:
        return work[:order, order:order + count]
    return work[:order, :order]


def chain(modes, batches, batch, span, start_ref, core_ref, mix_ref, upper_ref, captured_ref,
          state, squared_ref, work):
    state[...] = start_ref[:modes, :]
    energy = dot_nt(core_ref[...], core_ref[...])
    window_at = span + modes
    window = captured_ref.shape[2]
    for b in range(batches):
        at = window_at + batch * b
        base = modes + batch * b
        projected = state[:, at:at + batch]
        residual = start_ref[base:base + batch, :] - dot_nn(projected.T, state[...])
        against = dot_nt(residual[:, span:2 * span], state[:, :span])
        gram = residual[:, at:at + batch] - dot_nn(against, projected)
        upper, inverse = factor_block(gram)
        orthogonal = dot_nn(inverse, residual)
        squared_ref[:modes, :modes] = energy + dot_nt(projected, projected)
        squared_ref[:modes, modes:] = dot_nt(projected, upper)
        squared_ref[modes:, :modes] = dot_nt(upper, projected)
        squared_ref[modes:, modes:] = dot_nt(upper, upper)
        turned = squared_ref[:modes, :]
        for turn in range(TURNS):
            if turn:
                turned = dot_nn(turned, squared_ref[...])
            turned = factor_solve(dot_nt(turned, turned), turned, work)
        energy = dot_nt(dot_nn(turned, squared_ref[...]), turned)
        state[...] = dot_nn(turned[:, :modes], state[...]) + dot_nn(turned[:, modes:], orthogonal)
        captured_ref[b] = state[:, window_at:window_at + window]
    mix_ref[...] = state[:, :span]
    upper_ref[...] = factor_solve(energy, None, work, keep_factor=True)


def exchange(part_ref, out_ref, from_sub, half, from_z, quarter, from_y, slice_, from_x, full,
             send_sems, recv_sems):
    space = lax.axis_index("space")
    sub = lax.axis_index("sub")
    x, y, z = space // 16, (space // 4) % 4, space % 4
    other = (space, 1 - sub)

    def on_z(d):
        at = (z + d) % 4
        return at, (x * 16 + y * 4 + at, sub)

    def on_y(d):
        at = (y + d) % 4
        return at, (x * 16 + at * 4 + z, sub)

    def on_x(d):
        at = (x + d) % 4
        return at, (at * 16 + y * 4 + z, sub)

    barrier = pltpu.get_barrier_semaphore()
    partners = [other] + [line(d)[1] for line in (on_z, on_y, on_x) for d in (1, 2, 3)]
    for partner in partners:
        pl.semaphore_signal(
            barrier, inc=1, device_id=partner, device_id_type=pl.DeviceIdType.MESH
        )
    pl.semaphore_wait(barrier, len(partners))

    def send(src, dst, number, device):
        copy = pltpu.make_async_remote_copy(
            src_ref=src,
            dst_ref=dst,
            send_sem=send_sems.at[number],
            recv_sem=recv_sems.at[number],
            device_id=device,
            device_id_type=pl.DeviceIdType.MESH,
        )
        copy.start()
        return copy

    def rows(start, count):
        return pl.ds(pl.multiple_of(start, count), count)

    rows_sub = out_ref.shape[0] // 2
    rows_z, rows_y, rows_x = rows_sub // 4, rows_sub // 16, rows_sub // 64
    send(part_ref.at[rows((1 - sub) * rows_sub, rows_sub)], from_sub, 0, other).wait()
    half[...] = part_ref[rows(sub * rows_sub, rows_sub), :] + from_sub[...]
    number = 1
    for line, place, source, count, landing, target in (
        (on_z, z, half, rows_z, from_z, quarter),
        (on_y, y, quarter, rows_y, from_y, slice_),
        (on_x, x, slice_, rows_x, from_x, None),
    ):
        copies = []
        for d in (1, 2, 3):
            at, device = line(d)
            copies.append(send(source.at[rows(at * count, count)], landing.at[d - 1], number, device))
            number += 1
        for copy in copies:
            copy.wait()
        total = source[rows(place * count, count), :] + landing[0] + landing[1] + landing[2]
        if target is None:
            base = sub * rows_sub + z * rows_z + y * rows_y + x * rows_x
            full[rows(base, count), :] = total
        else:
            target[...] = total
    for line, count, base in (
        (on_x, rows_x, sub * rows_sub + z * rows_z + y * rows_y + x * rows_x),
        (on_y, rows_y, sub * rows_sub + z * rows_z + y * rows_y),
        (on_z, rows_z, sub * rows_sub + z * rows_z),
    ):
        mine = full.at[rows(base, count)]
        copies = []
        for d in (1, 2, 3):
            copies.append(send(mine, mine, number, line(d)[1]))
            number += 1
        for copy in copies:
            copy.wait()
    mine = full.at[rows(sub * rows_sub, rows_sub)]
    send(mine, mine, number, other).wait()
    out_ref[...] = full[...]


def sum_over_devices(packed):
    total, lanes = packed.shape
    part = total // 2

    def scratch(*shape):
        return pltpu.VMEM(shape + (lanes,), jnp.float32)

    vmem = pl.BlockSpec(memory_space=pltpu.VMEM)
    return pl.pallas_call(
        exchange,
        out_shape=jax.ShapeDtypeStruct(packed.shape, jnp.float32),
        in_specs=[vmem],
        out_specs=vmem,
        scratch_shapes=[
            scratch(part),
            scratch(part),
            scratch(3, part // 4),
            scratch(part // 4),
            scratch(3, part // 16),
            scratch(part // 16),
            scratch(3, part // 64),
            scratch(total),
            pltpu.SemaphoreType.DMA((20,)),
            pltpu.SemaphoreType.DMA((20,)),
        ],
        compiler_params=pltpu.CompilerParams(collective_id=0, has_side_effects=True),
        name="exchange",
    )(packed)


def body(mode_rows, snapshots, probe_fields, core_factor):
    modes, local_rows = mode_rows.shape
    batches, batch = snapshots.shape[:2]
    probes = probe_fields.shape[0]
    volume = 1.0 / (local_rows * lax.axis_size("space") * lax.axis_size("sub"))
    taken = batches * batch
    flat = snapshots.reshape(taken, local_rows)

    def inner(left, right):
        return lax.dot_general(left, right, (((1,), (1,)), ((), ())), precision=SPLIT)

    uu = inner(mode_rows, mode_rows)
    uc = inner(mode_rows, flat)
    up = inner(mode_rows, probe_fields)
    cc = inner(flat, flat)
    cp = inner(flat, probe_fields)
    rest = taken - 128
    pair = jnp.concatenate(
        [uc[:, 128:], jnp.pad(cc[:, 128:], ((0, modes - taken), (0, 0)))], axis=1
    )
    pieces = [uu[:, :128], uu[:, 128:], uc[:, :128], up, pair, cc[:, :128], cp]
    used = sum(piece.shape[0] for piece in pieces)
    packed = jnp.concatenate(
        pieces + [jnp.zeros((-used % 1024, 128), jnp.float32)], axis=0
    )
    summed = sum_over_devices(packed)
    back = []
    at = 0
    for piece in pieces:
        back.append(summed[at:at + piece.shape[0], :])
        at += piece.shape[0]
    uu = jnp.concatenate(back[:2], axis=1)
    uc = jnp.concatenate([back[2], back[4][:, :rest]], axis=1)
    up = back[3]
    cc = jnp.concatenate([back[5], back[4][:taken, rest:]], axis=1)
    cp = back[6]
    total = modes + taken
    span = -(-total // 128) * 128
    gram = jnp.concatenate(
        [
            jnp.concatenate([uu, uc, up], axis=1),
            jnp.concatenate([uc.T, cc, cp], axis=1),
        ],
        axis=0,
    ) * volume
    width = -(-(total + probes) // 128) * 128
    start = jnp.concatenate(
        [
            jnp.eye(total, span, dtype=jnp.float32),
            jnp.pad(gram, ((0, 0), (0, width - total - probes))),
        ],
        axis=1,
    )
    vmem = pl.BlockSpec(memory_space=pltpu.VMEM)
    mix, upper, captured = pl.pallas_call(
        lambda *refs: chain(modes, batches, batch, span, *refs),
        out_shape=(
            jax.ShapeDtypeStruct((modes, span), jnp.float32),
            jax.ShapeDtypeStruct((modes, modes), jnp.float32),
            jax.ShapeDtypeStruct((batches, modes, taken + probes), jnp.float32),
        ),
        in_specs=[vmem, vmem],
        out_specs=(vmem, vmem, vmem),
        scratch_shapes=[
            pltpu.VMEM((modes, span + width), jnp.float32),
            pltpu.VMEM((modes + batch, modes + batch), jnp.float32),
            pltpu.VMEM((modes, 2 * modes + batch), jnp.float32),
        ],
        name="chain",
    )(start, core_factor)
    new_modes = jnp.dot(mix[:, :modes], mode_rows, precision=SPLIT) + jnp.dot(
        mix[:, modes:total], flat, precision=SPLIT
    )
    return (new_modes, upper.T, captured)


def solution(mesh):
    return jax.shard_map(
        body,
        mesh=mesh,
        in_specs=(
            P(None, AXES),
            P(None, None, AXES),
            P(None, AXES),
            P(),
        ),
        out_specs=(P(None, AXES), P(), P()),
        check_vma=False,
    )
```
